32 devices in a mesh: dp: 8 (over z, y), ns: 4 (over x, core).
Axes of the slice: x: 2, y: 2, z: 4, core: 2. Of those that a mesh axis runs over, the one named last changes fastest.
Arguments:
- patches: bfloat16 [32768, 768], P(('dp', 'ns')), may hold values from -6 to 6
- masked: int32 [32768], P(('dp', 'ns')), may hold values from 0 to 1, as said below
- counts: int32 [32], P(('dp', 'ns')), may hold values from 64 to 1024, as said below
- hog_targets: bfloat16 [108, 32768], P(None, ('dp', 'ns')), may hold values from -6 to 6
- qkv_weight: float32 [768, 2304], P(None, ('dp', 'ns')), may hold values from -0.3125 to 0.3125
- out_weight: float32 [768, 768], P(('dp', 'ns')), may hold values from -1.25 to 1.25
- fc1_weight: float32 [768, 3072], P(None, ('dp', 'ns')), may hold values from -0.21875 to 0.21875
- fc2_weight: float32 [3072, 768], P(('dp', 'ns')), may hold values from -0.109375 to 0.109375
- head_weight: float32 [768, 108], P(('dp', 'ns')), may hold values from -0.21875 to 0.21875
- vectors: float32 [13, 768], P(None, ('dp', 'ns')), may hold values from -4 to 4
- qkv_moment: float32 [768, 2304], P(None, ('dp', 'ns')), may hold values from -0.001953125 to 0.001953125
- out_moment: float32 [768, 768], P(('dp', 'ns')), may hold values from -0.001953125 to 0.001953125
- fc1_moment: float32 [768, 3072], P(None, ('dp', 'ns')), may hold values from -0.001953125 to 0.001953125
- fc2_moment: float32 [3072, 768], P(('dp', 'ns')), may hold values from -0.001953125 to 0.001953125
- head_first: float32 [768, 108], P(('dp', 'ns')), may hold values from -0.00024414062 to 0.00024414062
- head_second: float32 [768, 108], P(('dp', 'ns')), may hold values from 8.3789145e-09 to 3.072269e-08
- vector_first: float32 [13, 768], P(None, ('dp', 'ns')), may hold values from -0.0007324219 to 0.0007324219
- vector_second: float32 [13, 768], P(None, ('dp', 'ns')), may hold values from 6.982429e-08 to 2.7929715e-07
Outputs:
- block_output: bfloat16 [32768, 768], P(('dp', 'ns'))
- patch_grads: float32 [32768, 768], P(('dp', 'ns'))
- grad_norm: float32 [], replicated
- qkv_moment_new: float32 [768, 2304], P(None, ('dp', 'ns'))
- out_moment_new: float32 [768, 768], P(('dp', 'ns'))
- fc1_moment_new: float32 [768, 3072], P(None, ('dp', 'ns'))
- fc2_moment_new: float32 [3072, 768], P(('dp', 'ns'))
- qkv_new: float32 [768, 2304], P(None, ('dp', 'ns'))
- out_new: float32 [768, 768], P(('dp', 'ns'))
- fc1_new: float32 [768, 3072], P(None, ('dp', 'ns'))
- fc2_new: float32 [3072, 768], P(('dp', 'ns'))
- qkv_copy: bfloat16 [768, 2304], P(None, ('dp', 'ns'))
- out_copy: bfloat16 [768, 768], P(('dp', 'ns'))
- fc1_copy: bfloat16 [768, 3072], P(None, ('dp', 'ns'))
- fc2_copy: bfloat16 [3072, 768], P(('dp', 'ns'))
- head_first_new: float32 [768, 108], P(('dp', 'ns'))
- head_second_new: float32 [768, 108], P(('dp', 'ns'))
- head_new: float32 [768, 108], P(('dp', 'ns'))
- head_copy: bfloat16 [768, 108], P(('dp', 'ns'))
- vector_first_new: float32 [13, 768], P(None, ('dp', 'ns'))
- vector_second_new: float32 [13, 768], P(None, ('dp', 'ns'))
- vectors_new: float32 [13, 768], P(None, ('dp', 'ns'))
- vectors_copy: bfloat16 [13, 768], P(None, ('dp', 'ns'))
The draws below stay inside these ranges and needn't reach their ends.
Inputs may be any that keep to these rules, and one draw needn't show every extreme that they name: The first slot of every image is masked. `counts`: an image's valid patches are its first slots; in every draw some image has all 1024 slots valid.
All inputs are finite; a program needn't handle non-finite values.
Results may differ from the reference program's by a relative error of at most 0.006.
The reference program's roundings to bfloat16 on the way count: a program that leaves them out, or rounds other values in their place, can miss the bound.
Values may be sent and summed in bfloat16 or wider, within the bound.
A program may use at most 320 MiB of HBM per device.

```python
import math
from functools import partial
import jax
import jax.numpy as jnp
from jax import lax

D = 768
HEADS = 12
HEAD_DIM = 64
FF = 3072
HOG = 108
SEQ = 1024
IMAGES = 32
SLOTS = 32768
NVEC = 13


def draw_masked(key, part):
    pick_draw = jax.random.randint(key, (SLOTS,), 0, 5)
    first_slot = jnp.arange(SLOTS) % SEQ == 0
    return jnp.where(jnp.logical_or(first_slot, pick_draw < 2), 1, 0).astype(jnp.int32)


def draw_counts(key, part):
    level_key, chosen_key = jax.random.split(key)
    level_draw = jax.random.randint(level_key, (IMAGES,), 0, 31)
    chosen = jax.random.randint(chosen_key, (), 0, IMAGES)
    level_draw = jnp.where(jnp.arange(IMAGES) == chosen, 30, level_draw)
    floor_count = SEQ // 16
    return (floor_count + level_draw * level_draw * (SEQ - floor_count) // 900).astype(jnp.int32)


def draw_vectors(key, part):
    base_draw = jnp.clip(jax.random.normal(key, (NVEC, D), jnp.float32), -4.0, 4.0)
    row_index = jnp.arange(NVEC)[:, None]
    gain_rows = jnp.logical_or(row_index == 0, row_index == 5)
    token_row = row_index == 8
    spread = jnp.where(token_row, 1.0, jnp.where(gain_rows, 0.15, 0.3))
    return jnp.where(gain_rows, 1.0, 0.0) + spread * base_draw


def block_scale(key, extent, cuts, smallest, high):
    def one(dim, shards_of):
        steps = jax.random.uniform(jax.random.fold_in(jax.random.fold_in(key, 6), dim), (shards_of,), jnp.float32, smallest / len(cuts), high / len(cuts))
        return jnp.repeat(jnp.exp(steps), extent[dim] // shards_of).reshape((-1,) + (1,) * (len(extent) - dim - 1))

    loudness = one(*cuts[0])
    for cut in cuts[1:]:
        loudness = loudness * one(*cut)
    return loudness


def gaussian(rng, shape, scale, most, cuts=(), held_as=jnp.bfloat16):
    level = block_scale(rng, shape, cuts, -0.22, 0.18) if cuts else 1.0
    drawn = jax.random.normal(rng, shape, jnp.float32) * scale * level
    return jnp.minimum(jnp.maximum(drawn, -most), most).astype(held_as)


def setup_inputs(seed: int = 0) -> dict:
    seeds = jax.random.split(jax.random.key(seed), 19)
    patches = gaussian(seeds[0], (SLOTS, D), 1.0, 6.0, ((0, 32),))
    masked = draw_masked(jax.random.fold_in(seeds[18], 71), 0)
    counts = draw_counts(jax.random.fold_in(seeds[18], 71), 0)
    hog_targets = gaussian(seeds[3], (HOG, SLOTS), 1.0, 6.0, ((1, 32),))
    qkv_weight = gaussian(seeds[4], (D, 3 * D), (D // 2) ** -0.5, 0.3125, ((1, 32),), jnp.float32)
    out_weight = gaussian(seeds[5], (D, D), (D // 32) ** -0.5, 1.25, ((0, 32),), jnp.float32)
    fc1_weight = gaussian(seeds[6], (D, FF), D ** -0.5, 0.21875, ((1, 32),), jnp.float32)
    fc2_weight = gaussian(seeds[7], (FF, D), FF ** -0.5, 0.109375, ((0, 32),), jnp.float32)
    head_weight = gaussian(seeds[8], (D, HOG), D ** -0.5, 0.21875, ((0, 32),), jnp.float32)
    vectors = draw_vectors(jax.random.fold_in(seeds[18], 71), 0)
    qkv_moment = gaussian(seeds[10], (D, 3 * D), ((4 * D * D + 2 * D * FF + D * HOG) ** -0.5), 0.001953125, ((1, 32),), jnp.float32)
    out_moment = gaussian(seeds[11], (D, D), ((4 * D * D + 2 * D * FF + D * HOG) ** -0.5), 0.001953125, ((0, 32),), jnp.float32)
    fc1_moment = gaussian(seeds[12], (D, FF), ((4 * D * D + 2 * D * FF + D * HOG) ** -0.5), 0.001953125, ((1, 32),), jnp.float32)
    fc2_moment = gaussian(seeds[13], (FF, D), ((4 * D * D + 2 * D * FF + D * HOG) ** -0.5), 0.001953125, ((0, 32),), jnp.float32)
    head_first = gaussian(seeds[14], (D, HOG), (0.11 * (4 * D * D + 2 * D * FF + D * HOG) ** -0.5), 0.00024414062, ((0, 32),), jnp.float32)
    head_second = jnp.clip(jnp.exp(math.log(3.072268839332537e-08) - 1.299283 * jax.random.uniform(seeds[15], (D, HOG), jnp.float32) ** block_scale(seeds[15], (D, HOG), ((0, 32),), -0.2, 0.2)), 8.378914451157016e-09, 3.072268839332537e-08)
    vector_first = gaussian(seeds[16], (NVEC, D), (0.33 * (4 * D * D + 2 * D * FF + D * HOG) ** -0.5), 0.0007324219, ((1, 32),), jnp.float32)
    vector_second = jnp.clip(jnp.exp(math.log(2.7929715429309e-07) - 1.3862944 * jax.random.uniform(seeds[17], (NVEC, D), jnp.float32) ** block_scale(seeds[17], (NVEC, D), ((1, 32),), -0.2, 0.2)), 6.98242885732725e-08, 2.7929715429309e-07)
    return dict(patches=patches, masked=masked, counts=counts, hog_targets=hog_targets, qkv_weight=qkv_weight, out_weight=out_weight, fc1_weight=fc1_weight, fc2_weight=fc2_weight, head_weight=head_weight, vectors=vectors, qkv_moment=qkv_moment, out_moment=out_moment, fc1_moment=fc1_moment, fc2_moment=fc2_moment, head_first=head_first, head_second=head_second, vector_first=vector_first, vector_second=vector_second)


@jax.custom_vjp
def low(v):
    return lax.optimization_barrier(v.astype(jnp.bfloat16)).astype(jnp.float32)

@jax.custom_vjp
def low_back(v):
    return v

def low_keep(v):
    return (low(v), None)

def low_pass(kept, grad):
    return (grad,)

def back_keep(v):
    return (v, None)

def back_low(kept, grad):
    return (low(grad),)
low.defvjp(low_keep, low_pass)
low_back.defvjp(back_keep, back_low)
newton_first = 3.4445
newton_second = -4.775
newton_third = 2.0315
muon_rate = 0.5
muon_decay = 0.01
momentum_keep = 0.5
beta_first = 0.9
beta_second = 0.95
head_rate = 0.1
head_decay = 0.01
vector_rate = 0.3
highest = lax.Precision.HIGHEST

def layer_norm(row_data, gain, shift):
    center = row_data - lax.optimization_barrier(jnp.mean(row_data, axis=-1, keepdims=True))
    spread = lax.optimization_barrier(jnp.mean(center * center, axis=-1, keepdims=True))
    return center * lax.rsqrt(spread + 1e-06) * gain + shift

def high_dot(left, right):
    return jnp.dot(left, right, precision=highest)

def image_loss(params, item):
    qkv_low, out_low, fc1_low, fc2_low, head_low, vector_rows = params
    patch_rows, mask_rows, live_count, hog_cols = item
    slot_count = patch_rows.shape[0]
    model_width = out_low.shape[0]
    live_mask = jnp.arange(slot_count) < live_count
    masked_here = mask_rows == 1
    chosen = jnp.logical_and(masked_here, live_mask).astype(jnp.float32)
    stream = jnp.where(masked_here[:, None], vector_rows[8][None, :], patch_rows)
    input_one = low(layer_norm(stream, vector_rows[0], vector_rows[1]))
    qkv_bias = jnp.concatenate([vector_rows[2], jnp.zeros_like(vector_rows[2]), vector_rows[3]])
    joined = low_back(low(high_dot(input_one, qkv_low) + qkv_bias))
    queries = joined[:, :model_width].reshape(slot_count, HEADS, HEAD_DIM)
    key_rows = joined[:, model_width:2 * model_width].reshape(slot_count, HEADS, HEAD_DIM)
    value_rows = joined[:, 2 * model_width:].reshape(slot_count, HEADS, HEAD_DIM)
    scores = low_back(jnp.einsum('qhe,khe->hqk', queries, key_rows, precision=highest) * 0.125)
    scores = jnp.where(live_mask[None, None, :], scores, -1e+30)
    attn_weights = low(jax.nn.softmax(scores, axis=-1))
    mixture = jnp.einsum('hqk,khe->qhe', attn_weights, value_rows, precision=highest).reshape(slot_count, model_width)
    mixture = low_back(low(mixture))
    after_attn = stream + low_back(high_dot(mixture, out_low) + vector_rows[4])
    input_two = low(layer_norm(after_attn, vector_rows[5], vector_rows[6]))
    pre_act = low_back(high_dot(input_two, fc1_low) + vector_rows[9:].reshape(-1))
    activation = low(jax.nn.gelu(pre_act, approximate=False))
    after_mlp = after_attn + low_back(high_dot(activation, fc2_low) + vector_rows[7])
    hidden = low(after_mlp)
    predicted = low_back(jnp.einsum('dh,td->ht', head_low, hidden, precision=highest))
    misfit = predicted - hog_cols
    per_slot = lax.optimization_barrier(jnp.sum(misfit * misfit, axis=0))
    return (jnp.sum(per_slot * chosen) / jnp.sum(chosen), hidden)

def orthogonalize(matrix):
    frobenius = jnp.sqrt(jnp.sum(matrix * matrix))
    iterate = matrix / (frobenius + 1e-07)
    for newton_turn in range(5):
        gram_matrix = jnp.dot(iterate.T, iterate, precision=highest)
        first_term = jnp.dot(iterate, gram_matrix, precision=highest)
        second_term = jnp.dot(first_term, gram_matrix, precision=highest)
        iterate = newton_first * iterate + newton_second * first_term + newton_third * second_term
    return iterate

def muon_update(weight, moment, grad_piece, shrink, wide_form):
    moment_new = momentum_keep * moment + shrink * grad_piece
    tall_form = moment_new.T if wide_form else moment_new
    ortho = orthogonalize(tall_form)
    ortho = ortho.T if wide_form else ortho
    factor = math.sqrt(max(1.0, tall_form.shape[0] / tall_form.shape[1]))
    weight_new = weight - muon_rate * (factor * ortho + muon_decay * weight)
    return (moment_new, weight_new)

def adam_update(weight, first_old, second_old, grad_piece, rate, decay):
    first_new = beta_first * first_old + (1.0 - beta_first) * grad_piece
    second_new = beta_second * second_old + (1.0 - beta_second) * grad_piece * grad_piece
    weight_new = weight - rate * (first_new / (jnp.sqrt(second_new) + 1e-08) + decay * weight)
    return (first_new, second_new, weight_new)

def reference(patches, masked, counts, hog_targets, qkv_weight, out_weight, fc1_weight, fc2_weight, head_weight, vectors, qkv_moment, out_moment, fc1_moment, fc2_moment, head_first, head_second, vector_first, vector_second):
    patch_images = patches.astype(jnp.float32).reshape(IMAGES, SEQ, D)
    mask_images = masked.reshape(IMAGES, SEQ)
    hog_images = jnp.transpose(hog_targets.astype(jnp.float32).reshape(HOG, IMAGES, SEQ), (1, 0, 2))

    def forward(qkv_full, out_full, fc1_full, fc2_full, head_full, vector_full, patch_full):
        params = (low(qkv_full), low(out_full), low(fc1_full), low(fc2_full), low(head_full), low(vector_full))
        per_image = jax.checkpoint(partial(image_loss, params))
        losses, hidden = lax.map(per_image, (patch_full, mask_images, counts, hog_images))
        return (jnp.sum(losses), hidden)
    loss_value, pullback, hidden = jax.vjp(forward, qkv_weight, out_weight, fc1_weight, fc2_weight, head_weight, vectors, patch_images, has_aux=True)
    grads = pullback(jnp.ones_like(loss_value))
    qkv_grad, out_grad, fc1_grad, fc2_grad, head_grad, vector_grad, patch_grad = grads
    every_grad = (qkv_grad, out_grad, fc1_grad, fc2_grad, head_grad, vector_grad)
    grad_norm = jnp.sqrt(jnp.sum(jnp.stack([jnp.sum(grad_piece * grad_piece) for grad_piece in every_grad])))
    shrink = jnp.minimum(1.0, 1.0 / (grad_norm + 1e-06))
    qkv_moment_new, qkv_new = muon_update(qkv_weight, qkv_moment, qkv_grad, shrink, True)
    out_moment_new, out_new = muon_update(out_weight, out_moment, out_grad, shrink, False)
    fc1_moment_new, fc1_new = muon_update(fc1_weight, fc1_moment, fc1_grad, shrink, True)
    fc2_moment_new, fc2_new = muon_update(fc2_weight, fc2_moment, fc2_grad, shrink, False)
    head_first_new, head_second_new, head_new = adam_update(head_weight, head_first, head_second, shrink * head_grad, head_rate, head_decay)
    vector_first_new, vector_second_new, vectors_new = adam_update(vectors, vector_first, vector_second, shrink * vector_grad, vector_rate, 0.0)
    block_output = hidden.reshape(SLOTS, D).astype(jnp.bfloat16)
    patch_grads = patch_grad.reshape(SLOTS, D)
    return (block_output, patch_grads, grad_norm, qkv_moment_new, out_moment_new, fc1_moment_new, fc2_moment_new, qkv_new, out_new, fc1_new, fc2_new, qkv_new.astype(jnp.bfloat16), out_new.astype(jnp.bfloat16), fc1_new.astype(jnp.bfloat16), fc2_new.astype(jnp.bfloat16), head_first_new, head_second_new, head_new, head_new.astype(jnp.bfloat16), vector_first_new, vector_second_new, vectors_new, vectors_new.astype(jnp.bfloat16))
```

```python
import functools
import math

import jax
import jax.numpy as jnp
from jax import lax
from jax.experimental import pallas as pl
from jax.experimental.pallas import tpu as pltpu
from jax.sharding import PartitionSpec as P

HEADS = 12
HEAD_DIM = 64
PAYLOAD = 48
STACK = 16
MESH = pl.DeviceIdType.MESH

newton_first = 3.4445
newton_second = -4.775
newton_third = 2.0315
muon_rate = 0.5
muon_decay = 0.01
momentum_keep = 0.5
beta_first = 0.9
beta_second = 0.95
head_rate = 0.1
head_decay = 0.01
vector_rate = 0.3
highest = lax.Precision.HIGHEST
half_type = jnp.bfloat16
both = ("dp", "ns")

def ring_place(index, count):
    high, odd = lax.div(index, 2), lax.rem(index, 2)
    return high + odd * (count - 1 - 2 * high)

def ring_index(place, count):
    late = lax.div(place, count // 2)
    return 2 * place + late * (2 * count - 1 - 4 * place)

class Peers:
    def __init__(self, n_dp, n_ns):
        self.n_dp, self.n_ns = n_dp, n_ns
        self.dp, self.ns = lax.axis_index("dp"), lax.axis_index("ns")
        place = ring_place(self.dp, n_dp)
        low = lax.rem(self.ns, 2)
        high = lax.rem(lax.div(self.ns, 2), 2)
        flips = (0, 1 - 2 * low, 2 - 4 * high)
        self.columns = [self.ns, self.ns + flips[1], self.ns + flips[2], self.ns + flips[1] + flips[2]]
        self.rows = {0: self.dp}
        for shift in range(-(n_dp // 2), (n_dp - 1) // 2 + 1):
            if shift:
                self.rows[shift] = ring_index(lax.rem(place + shift + n_dp, n_dp), n_dp)
        self.ways = {
            "right": (self.rows[1], self.ns),
            "left": (self.rows[-1], self.ns),
            "cross": (self.dp, self.columns[2]),
            "core": (self.dp, self.columns[1]),
        }

    def slot(self, shift, bit):
        return self.rows[shift] * self.n_ns + self.columns[bit]

    def device(self, way):
        return self.ways[way]

    def greet(self):
        barrier = pltpu.get_barrier_semaphore()
        for way in ("right", "left", "cross", "core"):
            pl.semaphore_signal(barrier, inc=1, device_id=self.device(way), device_id_type=MESH)
        pl.semaphore_wait(barrier, 4)

def routes(n_dp, mode):
    ring_first, dp_only = mode != "cross", mode == "dp"
    right, left = n_dp // 2, (n_dp - 1) // 2
    table = {}
    start = [("right", ("r", 1, 0)), ("left", ("l", 1, 0)), ("cross", ("x", 0, 2)), ("core", ("c", 0, 1))]
    if dp_only:
        start = start[:2]
    columns = (0,) if ring_first else (0, 2)

    def along(kind, step, bit):
        shift = -step if kind == "r" else step
        limit = right if kind == "r" else left
        out = []
        if step < limit:
            out.append(("right" if kind == "r" else "left", (kind, step + 1, bit)))
        if not dp_only:
            if ring_first:
                out.append(("cross", ("x", shift, 2)))
            out.append(("core", ("c", shift, bit ^ 1)))
        table[(kind, step, bit)] = (shift, bit, out)

    def crossed(shift):
        out = []
        if dp_only:
            return
        if not ring_first:
            out += [("right", ("r", 1, 2)), ("left", ("l", 1, 2))]
        out.append(("core", ("c", shift, 3)))
        table[("x", shift, 2)] = (shift, 2, out)

    for step in range(1, right + 2):
        if ring_first or step == 1:
            if step == 1:
                crossed(0)
            else:
                crossed(1 - step)
                if step - 1 <= left:
                    crossed(step - 1)
        for bit in columns:
            if step <= right:
                along("r", step, bit)
            if step <= left:
                along("l", step, bit)
    return start, table

def finals(n_dp, mode):
    if mode == "dp":
        return []
    right, left = n_dp // 2, (n_dp - 1) // 2
    shifts = [0]
    for step in range(1, right + 1):
        shifts.append(-step)
        if step <= left:
            shifts.append(step)
    return [(shift, bit) for shift in shifts for bit in (1, 3)]

def gather_kernel(n_dp, n_ns, orders, *refs):
    count = len(orders)
    blocks, outs = refs[:count], refs[count : 2 * count]
    send_sem, recv_sem, own_sem = refs[2 * count :]
    peers = Peers(n_dp, n_ns)
    peers.greet()
    sends = []
    plans = [routes(n_dp, order) for order in orders]
    names = []
    for (start, table), mode in zip(plans, orders):
        ids = {}
        for key in table:
            ids[key] = len(ids)
        for shift, bit in finals(n_dp, mode):
            ids[("c", shift, bit)] = len(ids)
        names.append(ids)

    def push(a, source, slot, way, name):
        copy = pltpu.make_async_remote_copy(
            src_ref=source,
            dst_ref=outs[a].at[slot],
            send_sem=send_sem.at[a, names[a][name]],
            recv_sem=recv_sem.at[a, names[a][name]],
            device_id=peers.device(way),
            device_id_type=MESH,
        )
        copy.start()
        sends.append(copy)

    def landed(a, slot, name):
        pltpu.make_async_remote_copy(
            src_ref=outs[a].at[slot],
            dst_ref=outs[a].at[slot],
            send_sem=send_sem.at[a, names[a][name]],
            recv_sem=recv_sem.at[a, names[a][name]],
            device_id=peers.device("core"),
            device_id_type=MESH,
        ).wait_recv()

    def slot_of(a, shift, bit):
        return peers.rows[shift] if orders[a] == "dp" else peers.slot(shift, bit)

    for a in range(count):
        for way, name in plans[a][0]:
            push(a, blocks[a], slot_of(a, 0, 0), way, name)
    local = [
        pltpu.make_async_copy(blocks[a], outs[a].at[slot_of(a, 0, 0)], own_sem.at[a])
        for a in range(count)
    ]
    for copy in local:
        copy.start()
    rows = [list(plan[1].items()) for plan in plans]
    for turn in range(max(len(row) for row in rows)):
        for a in range(count):
            if turn < len(rows[a]):
                name, (shift, bit, out) = rows[a][turn]
                slot = slot_of(a, shift, bit)
                landed(a, slot, name)
                for way, target in out:
                    push(a, outs[a].at[slot], slot, way, target)
    tails = [finals(n_dp, mode) for mode in orders]
    for turn in range(max(len(tail) for tail in tails)):
        for a in range(count):
            if turn < len(tails[a]):
                shift, bit = tails[a][turn]
                landed(a, slot_of(a, shift, bit), ("c", shift, bit))
    for copy in local:
        copy.wait()
    for copy in sends:
        copy.wait_send()

def all_gather(n_dp, n_ns, arrays, orders, collective_id):
    n_dev = n_dp * n_ns
    sizes = [n_dp if mode == "dp" else n_dev for mode in orders]
    return pl.pallas_call(
        functools.partial(gather_kernel, n_dp, n_ns, orders),
        out_shape=tuple(
            jax.ShapeDtypeStruct((size,) + a.shape, a.dtype) for size, a in zip(sizes, arrays)
        ),
        in_specs=[pl.BlockSpec(memory_space=pltpu.VMEM)] * len(arrays),
        out_specs=tuple(pl.BlockSpec(memory_space=pl.ANY) for _ in arrays),
        scratch_shapes=[
            pltpu.SemaphoreType.DMA((len(arrays), n_dev - 1)),
            pltpu.SemaphoreType.DMA((len(arrays), n_dev - 1)),
            pltpu.SemaphoreType.DMA((len(arrays),)),
        ],
        compiler_params=pltpu.CompilerParams(collective_id=collective_id, has_side_effects=True),
    )(*arrays)


def swap_kernel(n_ns, block_ref, out_ref, send_sem, recv_sem, own_sem):
    dp, ns = lax.axis_index("dp"), lax.axis_index("ns")
    others = [lax.rem(ns + step, n_ns) for step in range(1, n_ns)]
    barrier = pltpu.get_barrier_semaphore()
    for other in others:
        pl.semaphore_signal(barrier, inc=1, device_id=(dp, other), device_id_type=MESH)
    pl.semaphore_wait(barrier, n_ns - 1)
    copies = []
    for index, other in enumerate(others):
        copy = pltpu.make_async_remote_copy(
            src_ref=block_ref.at[other],
            dst_ref=out_ref.at[ns],
            send_sem=send_sem.at[index],
            recv_sem=recv_sem.at[index],
            device_id=(dp, other),
            device_id_type=MESH,
        )
        copy.start()
        copies.append(copy)
    own = pltpu.make_async_copy(block_ref.at[ns], out_ref.at[ns], own_sem)
    own.start()
    for index in range(n_ns - 1):
        sender = lax.rem(ns + n_ns - 1 - index, n_ns)
        pltpu.make_async_remote_copy(
            src_ref=block_ref.at[sender],
            dst_ref=out_ref.at[sender],
            send_sem=send_sem.at[index],
            recv_sem=recv_sem.at[index],
            device_id=(dp, sender),
            device_id_type=MESH,
        ).wait_recv()
    own.wait()
    for copy in copies:
        copy.wait_send()


def swap(n_ns, block, collective_id):
    return pl.pallas_call(
        functools.partial(swap_kernel, n_ns),
        out_shape=jax.ShapeDtypeStruct(block.shape, block.dtype),
        in_specs=[pl.BlockSpec(memory_space=pltpu.VMEM)],
        out_specs=pl.BlockSpec(memory_space=pltpu.VMEM),
        scratch_shapes=[
            pltpu.SemaphoreType.DMA((n_ns - 1,)),
            pltpu.SemaphoreType.DMA((n_ns - 1,)),
            pltpu.SemaphoreType.DMA,
        ],
        compiler_params=pltpu.CompilerParams(collective_id=collective_id, has_side_effects=True),
    )(block)


def nn(left, right):
    return lax.dot_general(left, right, (((1,), (0,)), ((), ())), preferred_element_type=jnp.float32)

def nt(left, right):
    return lax.dot_general(left, right, (((1,), (1,)), ((), ())), preferred_element_type=jnp.float32)

def erfc_tail(size):
    t = 1.0 / (1.0 + (0.3275911 * math.sqrt(0.5)) * size)
    poly = ((((1.061405429 * t - 1.453152027) * t + 1.421413741) * t - 0.284496736) * t + 0.254829592) * t
    return poly * jnp.exp(-0.5 * (size * size))

def gelu(value):
    size = jnp.abs(value)
    return jnp.maximum(value, 0.0) - (0.5 * size) * erfc_tail(size)

def gelu_slope(value):
    tail = 0.5 * erfc_tail(jnp.abs(value))
    cdf = jnp.where(value >= 0.0, 1.0 - tail, tail)
    return cdf + value * (jnp.exp(-0.5 * value * value) * (1.0 / math.sqrt(2.0 * math.pi)))

def center_rows(rows):
    scale = 1.0 / rows.shape[1]
    center = rows - jnp.sum(rows, axis=1, keepdims=True) * scale
    spread = jnp.sum(center * center, axis=1, keepdims=True) * scale
    inverse = lax.rsqrt(spread + 1e-06)
    return center * inverse, inverse

def norm_back(grad_rows, normed, inverse, gain):
    scale = 1.0 / grad_rows.shape[1]
    scaled = grad_rows * gain
    first_mean = jnp.sum(scaled, axis=1, keepdims=True) * scale
    second_mean = jnp.sum(scaled * normed, axis=1, keepdims=True) * scale
    return inverse * (scaled - first_mean - normed * second_mean)

def thirds(wide):
    high = wide.astype(half_type).astype(jnp.float32)
    rest = wide - high
    mid = rest.astype(half_type).astype(jnp.float32)
    return high, mid, rest - mid

def stack_row(row):
    high, mid, low = thirds(row)
    place = lax.broadcasted_iota(jnp.int32, (STACK, row.shape[1]), 0)
    tall = jnp.where(place == 0, high, jnp.where(place == 1, mid, jnp.where(place == 2, low, 0.0)))
    return tall.astype(half_type)

def row_nn(row, matrix):
    return jnp.sum(nn(stack_row(row), matrix), axis=0, keepdims=True)

def row_nt(row, matrix):
    return jnp.sum(nt(stack_row(row), matrix), axis=0, keepdims=True)

def stack_wide(wide):
    return jnp.concatenate([piece.astype(half_type) for piece in thirds(wide)], axis=0)

def wide_nn(wide, matrix):
    tall = nn(stack_wide(wide), matrix)
    n = wide.shape[0]
    return tall[:n] + tall[n : 2 * n] + tall[2 * n :]

def wide_nt(wide, matrix):
    tall = nt(stack_wide(wide), matrix)
    n = wide.shape[0]
    return tall[:n] + tall[n : 2 * n] + tall[2 * n :]

def model_kernel(block, counts_ref, patches_ref, mask_col_ref, mask_row_ref, hog_ref, vec_ref,
                 qkv_ref, out_ref, fc1_ref, fc2_ref, head_ref,
                 hidden_ref, patch_grad_ref, payload_ref, query_ref, input_ref,
                 in1, joined, mixture, value_ext, bias_ref, after_rep, pre_rep, act_rep, in2_rep, grad_one_ref):
    seq, width = patches_ref.shape
    ff = fc1_ref.shape[0]
    steps = seq // block
    ff_rows = ff // width

    def span(step):
        return pl.ds(pl.multiple_of(step * block, block), block)

    def vec(index):
        return vec_ref[pl.ds(index, 1), :]

    place_row = lax.broadcasted_iota(jnp.int32, (1, seq), 1)
    live_row = place_row < counts_ref[0]
    bias_ref[...] = jnp.where(live_row, 0.0, -1e30)

    def stream_of(where):
        return jnp.where(mask_col_ref[where, :] == 1, vec(8), patches_ref[where, :].astype(jnp.float32))

    def first_step(step, carry):
        where = span(step)
        normed, _ = center_rows(stream_of(where))
        rows = (normed * vec(0) + vec(1)).astype(half_type)
        in1[where, :] = rows
        for part in range(3):
            piece = nt(rows, qkv_ref[pl.ds(part * width, width), :])
            if part == 0:
                piece = piece + vec(2)
            if part == 2:
                piece = piece + vec(3)
            joined[where, pl.ds(part * width, width)] = piece.astype(half_type)
        return carry

    lax.fori_loop(0, steps, first_step, 0)
    lane = lax.broadcasted_iota(jnp.int32, (block, 128), 1)

    def pair_step(pair, carry):
        cols = pl.multiple_of(pair * 128, 128)
        values = joined[:, pl.ds(2 * width + cols, 128)]
        keys = joined[:, pl.ds(width + cols, 128)]

        def attend(step, inner):
            where = span(step)
            query = joined[where, pl.ds(cols, 128)] * jnp.asarray(0.125, half_type)
            parts = []
            for side in range(2):
                own = (lane < 64) if side == 0 else (lane >= 64)
                scores = nt(jnp.where(own, query, jnp.zeros_like(query)), keys) + bias_ref[...]
                raised = jnp.exp(scores - jnp.max(scores, axis=1, keepdims=True))
                weights = raised * (1.0 / jnp.sum(raised, axis=1, keepdims=True))
                parts.append(nn(weights.astype(half_type), values))
            mixture[where, pl.ds(cols, 128)] = jnp.where(lane < 64, parts[0], parts[1]).astype(half_type)
            return inner

        return lax.fori_loop(0, steps, attend, carry)

    lax.fori_loop(0, width // 128, pair_step, 0)

    def mlp_step(step, carry):
        where = span(step)
        rep = pl.ds(pl.multiple_of(step * 16, 16), 16)
        after = stream_of(where) + (nn(mixture[where, :], out_ref[...]) + vec(4))
        after_rep[rep, :] = after[:16]
        normed, _ = center_rows(after)
        rows = (normed * vec(5) + vec(6)).astype(half_type)
        in2_rep[rep, :] = rows[:16]
        total = after + vec(7)
        for part in range(ff_rows):
            chunk = pl.ds(part * width, width)
            pre = nt(rows, fc1_ref[chunk, :]) + vec(9 + part)
            pre_rep[rep, chunk] = pre[:16]
            act = gelu(pre).astype(half_type)
            act_rep[rep, chunk] = act[:16]
            total = total + nn(act, fc2_ref[chunk, :])
        hidden_ref[where, :] = total.astype(half_type)
        return carry

    lax.fori_loop(0, steps, mlp_step, 0)

    hid_rep = hidden_ref[pl.ds(0, 16), :][:1].astype(jnp.float32)
    chosen = jnp.logical_and(mask_row_ref[...] == 1, live_row).astype(jnp.float32)
    count = jnp.sum(chosen, axis=1, keepdims=True)
    targets = row_nt(chosen, hog_ref[...])
    predicted = row_nn(hid_rep, head_ref[...])
    hog = hog_ref.shape[0]
    grad_pred = 2.0 * (predicted[:, :hog] - targets / count)
    grad_pred = jnp.concatenate([grad_pred, jnp.zeros((1, head_ref.shape[1] - hog), jnp.float32)], axis=1)
    grad_stream = row_nt(grad_pred, head_ref[...])
    grad_act = row_nt(grad_stream, fc2_ref[...])
    grad_pre = grad_act * gelu_slope(pre_rep[pl.ds(0, 16), :][:1])
    grad_two = row_nn(grad_pre, fc1_ref[...])
    norm_two, inverse_two = center_rows(after_rep[pl.ds(0, 16), :][:1])
    grad_attn = grad_stream + norm_back(grad_two, norm_two, inverse_two, vec(5))
    grad_mix = row_nt(grad_attn, out_ref[...])

    head_of = lax.broadcasted_iota(jnp.int32, (STACK, width), 1) // HEAD_DIM
    head_row = lax.broadcasted_iota(jnp.int32, (STACK, width), 0)
    own_head = head_of == head_row
    keys = joined[:, pl.ds(width, width)]
    values = joined[:, pl.ds(2 * width, width)]
    query_rep = joined[pl.ds(0, 16), pl.ds(0, width)][:1].astype(jnp.float32)
    query_heads = jnp.where(own_head, query_rep, 0.0)
    mix_heads = jnp.where(own_head, grad_mix, 0.0)
    scores = nt(query_heads.astype(half_type), keys) * 0.125 + bias_ref[...]
    raised = jnp.exp(scores - jnp.max(scores, axis=1, keepdims=True))
    probs = raised / jnp.sum(raised, axis=1, keepdims=True)
    probs_low = probs.astype(half_type)
    grad_probs = wide_nt(mix_heads, values)
    inner_sum = jnp.sum(probs * grad_probs, axis=1, keepdims=True)
    grad_scores = probs * (grad_probs - inner_sum)
    ds_high, ds_mid, ds_low = thirds(grad_scores)
    ds_stack = stack_wide(grad_scores)
    tall = nn(ds_stack, keys)
    grad_query = jnp.sum(
        jnp.where(own_head, tall[:16] + tall[16:32] + tall[32:], 0.0), axis=0, keepdims=True
    ) * 0.125
    sides = nn(jnp.concatenate([ds_stack, probs_low], axis=0), in1[...])
    key_side = sides[:16] + sides[16:32] + sides[32:48]
    value_side = sides[48:]
    key_back = nn(query_heads.astype(half_type), qkv_ref[pl.ds(width, width), :]) * 0.125
    value_back = wide_nn(mix_heads, qkv_ref[pl.ds(2 * width, width), :])
    query_back = row_nn(grad_query, qkv_ref[pl.ds(0, width), :])
    kb_high, kb_mid, _ = thirds(key_back)
    vb_high, vb_mid, _ = thirds(value_back)
    probs_wide = probs_low.astype(jnp.float32)
    slab = jnp.concatenate(
        [ds_high, ds_high, ds_mid, probs_wide, probs_wide, jnp.zeros((48, seq), jnp.float32)], axis=0
    )
    turned = slab.T.astype(half_type)
    backs = jnp.concatenate(
        [kb_high, kb_mid, kb_high, vb_high, vb_mid, jnp.zeros((48, width), jnp.float32)], axis=0
    ).astype(half_type)
    for part in range(steps):
        grad_one_ref[pl.ds(part * block, block), :] = nn(turned[part * block : (part + 1) * block], backs)

    def last_step(step, carry):
        gain_sum, shift_sum, rep_sum = carry
        where = span(step)
        normed, inverse = center_rows(stream_of(where))
        grad_one = grad_one_ref[where, :]
        mask = mask_col_ref[where, :] == 1
        patch_grad_ref[where, :] = jnp.where(mask, 0.0, norm_back(grad_one, normed, inverse, vec(0)))
        gain_sum = gain_sum + jnp.sum(grad_one * normed, axis=0, keepdims=True)
        shift_sum = shift_sum + jnp.sum(grad_one, axis=0, keepdims=True)
        rep_sum = rep_sum + jnp.sum(jnp.where(mask, grad_one, 0.0), axis=0, keepdims=True)
        return gain_sum, shift_sum, rep_sum

    zero = jnp.zeros((1, width), jnp.float32)
    gain_sum, shift_sum, rep_sum = lax.fori_loop(0, steps, last_step, (zero, zero, zero))
    norm_one, inverse_one = center_rows(vec(8))
    grad_gain = gain_sum + query_back * norm_one
    grad_shift = shift_sum + query_back
    grad_token = grad_attn + norm_back(rep_sum + query_back, norm_one, inverse_one, vec(0))
    weight_sum = jnp.sum(probs_wide, axis=1, keepdims=True)
    value_bias = jnp.sum(jnp.where(own_head, weight_sum, 0.0), axis=0, keepdims=True) * grad_mix
    act_row = act_rep[pl.ds(0, 16), :][:1].astype(jnp.float32)
    pieces = [
        hid_rep,
        jnp.concatenate([grad_pred, jnp.zeros((1, width - grad_pred.shape[1]), jnp.float32)], axis=1),
    ]
    pieces += [act_row[:, part * width : (part + 1) * width] for part in range(ff_rows)]
    pieces += [grad_stream, in2_rep[pl.ds(0, 16), :][:1].astype(jnp.float32)]
    pieces += [grad_pre[:, part * width : (part + 1) * width] for part in range(ff_rows)]
    pieces += [mixture[pl.ds(0, 16), :][:1].astype(jnp.float32), grad_attn, grad_query, grad_mix]
    pieces += [key_side[:HEADS], value_side[:HEADS]]
    pieces += [grad_gain, grad_shift, grad_two * norm_two, grad_two, grad_token, value_bias]
    rows = sum(piece.shape[0] for piece in pieces)
    pieces += [jnp.zeros((PAYLOAD - rows, width), jnp.float32)]
    payload_ref[...] = jnp.concatenate(pieces, axis=0).astype(payload_ref.dtype)
    query_ref[...] = query_rep
    input_ref[...] = in1[pl.ds(0, 16), :][:1].astype(jnp.float32)

def run_model(counts, patches, mask_col, mask_row, hog, vec, qkv, out, fc1, fc2, head, block=256):
    seq, width = patches.shape
    ff = fc1.shape[0]
    vm = pl.BlockSpec(memory_space=pltpu.VMEM)
    rep = (seq // block) * 16
    return pl.pallas_call(
        functools.partial(model_kernel, block),
        out_shape=(
            jax.ShapeDtypeStruct((seq, width), half_type),
            jax.ShapeDtypeStruct((seq, width), jnp.float32),
            jax.ShapeDtypeStruct((PAYLOAD, width), half_type),
            jax.ShapeDtypeStruct((1, width), jnp.float32),
            jax.ShapeDtypeStruct((1, width), jnp.float32),
        ),
        in_specs=[pl.BlockSpec(memory_space=pltpu.SMEM)] + [vm] * 10,
        out_specs=(vm,) * 5,
        scratch_shapes=[
            pltpu.VMEM((seq, width), half_type),
            pltpu.VMEM((seq, 3 * width), half_type),
            pltpu.VMEM((seq, width), half_type),
            pltpu.VMEM((seq, 256), half_type),
            pltpu.VMEM((1, seq), jnp.float32),
            pltpu.VMEM((rep, width), jnp.float32),
            pltpu.VMEM((rep, ff), jnp.float32),
            pltpu.VMEM((rep, ff), half_type),
            pltpu.VMEM((rep, width), half_type),
            pltpu.VMEM((seq, width), jnp.float32),
        ],
        compiler_params=pltpu.CompilerParams(vmem_limit_bytes=63 * 1024 * 1024),
    )(counts, patches, mask_col, mask_row, hog, vec, qkv, out, fc1, fc2, head)


def put_split(ref, value, count, rows=slice(None)):
    for index in range(count):
        piece = value.astype(half_type)
        ref[index, rows, :] = piece
        if index + 1 < count:
            value = value - piece.astype(jnp.float32)

pairs_of = {3: ((0, 1), (1, 0), (0, 0)), 6: ((0, 2), (2, 0), (1, 1), (0, 1), (1, 0), (0, 0))}

def strip_product(left, right, passes, row, tile, col0, width):
    total = None
    for li, ri in pairs_of[passes]:
        part = jnp.dot(left[li, pl.ds(row, tile), :], right[ri, :, pl.ds(col0, width - col0)],
                       preferred_element_type=jnp.float32)
        total = part if total is None else total + part
    return total

def newton_kernel(sym, plan, gram_ref, out_ref, gram_s, poly_s, half_s, total_s, gram_f, work_f, poly_f):
    width = gram_ref.shape[0]
    tile = 256
    def product(left, right, dest, passes, post):
        for r in range(0, width, tile):
            c0 = r if sym else 0
            blk = strip_product(left, right, passes, r, tile, c0, width)
            dest[pl.ds(r, tile), pl.ds(c0, width - c0)] = post(blk, r, c0)
        if sym:
            for r in range(0, width, tile):
                for c in range(r + tile, width, tile):
                    dest[pl.ds(c, tile), pl.ds(r, tile)] = dest[pl.ds(r, tile), pl.ds(c, tile)].T
    gram_f[...] = gram_ref[...]
    for turn in range(5):
        p1 = plan[turn]
        n = 3 if p1 == 6 else 2
        put_split(gram_s, gram_f[...], n)
        def poly_post(blk, r, c0):
            g = gram_f[pl.ds(r, tile), pl.ds(c0, width - c0)]
            rows = lax.broadcasted_iota(jnp.int32, blk.shape, 0) + r
            cols = lax.broadcasted_iota(jnp.int32, blk.shape, 1) + c0
            return newton_third * blk + newton_second * g + jnp.where(rows == cols, newton_first, 0.0)
        product(gram_s, gram_s, poly_f, p1, poly_post)
        put_split(poly_s, poly_f[...], n)
        same = lambda blk, r, c0: blk
        if turn == 0:
            put_split(total_s, poly_f[...], 2)
        else:
            product(total_s, poly_s, work_f, 3, same)
            if turn < 4:
                put_split(total_s, work_f[...], 2)
            else:
                out_ref[...] = work_f[...]
        if turn < 4:
            product(poly_s, gram_s, work_f, p1, same)
            put_split(half_s, work_f[...], n)
            product(half_s, poly_s, gram_f, p1, same)

def newton(gram, sym=True, plan=(6,3,3,3,3)):
    w = gram.shape[0]
    return pl.pallas_call(
        functools.partial(newton_kernel, sym, plan),
        out_shape=jax.ShapeDtypeStruct((w, w), jnp.float32),
        in_specs=[pl.BlockSpec(memory_space=pltpu.VMEM)],
        out_specs=pl.BlockSpec(memory_space=pltpu.VMEM),
        scratch_shapes=[pltpu.VMEM((3, w, w), half_type)] * 3 + [pltpu.VMEM((2, w, w), half_type)]
        + [pltpu.VMEM((w, w), jnp.float32)] * 3,
        compiler_params=pltpu.CompilerParams(vmem_limit_bytes=60 * 1024 * 1024),
    )(gram)


def adam_update(weight, first_old, second_old, grad_piece, rate, decay):
    first_new = beta_first * first_old + (1.0 - beta_first) * grad_piece
    second_new = beta_second * second_old + (1.0 - beta_second) * grad_piece * grad_piece
    weight_new = weight - rate * (first_new / (jnp.sqrt(second_new) + 1e-08) + decay * weight)
    return (first_new, second_new, weight_new)


def exact(spec, left, right):
    return jnp.einsum(spec, left, right, precision=highest)


def local(
    n_dp,
    n_ns,
    patches,
    masked,
    counts,
    hog_targets,
    qkv_weight,
    out_weight,
    fc1_weight,
    fc2_weight,
    head_weight,
    vectors,
    qkv_moment,
    out_moment,
    fc1_moment,
    fc2_moment,
    head_first,
    head_second,
    vector_first,
    vector_second,
):
    n_dev = n_dp * n_ns
    me_dp = lax.axis_index("dp")
    me_ns = lax.axis_index("ns")
    me = me_dp * n_ns + me_ns
    width = patches.shape[1]
    hidden_units = fc1_weight.shape[1] * n_dev
    hog_rows = hog_targets.shape[0]
    seq_len = patches.shape[0]
    n_vec = vectors.shape[0]
    slot_rows = max(fc1_weight.shape[1], qkv_weight.shape[1], fc2_weight.shape[0])

    def slot(tall_piece):
        return jnp.pad(tall_piece, ((0, slot_rows - tall_piece.shape[0]), (0, 0)))

    qkv_block = qkv_weight.T.astype(half_type)
    vec_block = jnp.pad(
        vectors.astype(half_type), ((0, 16 - n_vec), (0, 128 - vectors.shape[1]))
    )
    qkv_slots, vec_slots = all_gather(
        n_dp, n_ns, (qkv_block, vec_block), ("cross", "ring"), 1
    )
    head_block = jnp.pad(head_weight.astype(half_type), ((0, 0), (0, 128 - hog_rows)))
    out_slots, fc1_slots, fc2_slots, head_slots = all_gather(
        n_dp,
        n_ns,
        (
            out_weight.astype(half_type),
            fc1_weight.T.astype(half_type),
            fc2_weight.astype(half_type),
            head_block,
        ),
        ("ring", "ring", "cross", "ring"),
        2,
    )
    my_moments = jnp.stack(
        [
            slot(piece.astype(half_type))
            for piece in (qkv_moment.T, out_moment, fc1_moment.T, fc2_moment)
        ]
    )
    swapped = swap(n_ns, my_moments, 3)
    (old_tall,) = all_gather(n_dp, n_ns, (swapped,), ("dp",), 4)
    old_tall = old_tall.reshape(n_dev, slot_rows, width)
    vec_rows = jnp.pad(
        vec_slots[:, :n_vec, : vectors.shape[1]].transpose(1, 0, 2).reshape(n_vec, width),
        ((0, 16 - n_vec), (0, 0)),
    ).astype(jnp.float32)
    hidden, patch_grads, payload, query_rep, input_rep = run_model(
        counts,
        patches,
        masked.reshape(seq_len, 1),
        masked.reshape(1, seq_len),
        hog_targets,
        vec_rows,
        qkv_slots.reshape(3 * width, width),
        out_slots.reshape(width, width),
        fc1_slots.reshape(hidden_units, width),
        fc2_slots.reshape(hidden_units, width),
        head_slots.reshape(width, 128),
    )
    (gathered,) = all_gather(n_dp, n_ns, (payload,), ("ring",), 5)
    gathered = gathered.astype(jnp.float32)
    query_rep = query_rep.reshape(HEADS, HEAD_DIM)
    input_rep = input_rep.reshape(width)
    ff_rows = hidden_units // width
    cursor = [0]

    def take(count):
        start = cursor[0]
        cursor[0] += count
        return gathered[:, start : start + count].reshape(n_dev, count * width)

    all_hid = take(1)
    all_pred = take(1)[:, :hog_rows]
    all_act = take(ff_rows)
    all_branch = take(1)
    all_two = take(1)
    all_pre = take(ff_rows)
    all_mix = take(1)
    all_attn = take(1)
    all_query = jnp.sum(take(1), axis=0)
    all_gmix = take(1)
    all_key = jnp.sum(take(HEADS).reshape(n_dev, HEADS, width), axis=0)
    all_value = take(HEADS).reshape(n_dev, HEADS, width)
    sums = jnp.sum(gathered[:, cursor[0] : cursor[0] + 6], axis=0)
    sum_one = jnp.sum(gathered[:, 2 + ff_rows], axis=0)
    vector_total = jnp.concatenate(
        [
            sums[0:2],
            all_query[None],
            sums[5:6],
            jnp.sum(all_attn, axis=0)[None],
            sums[2:4],
            sum_one[None],
            sums[4:5],
            jnp.sum(all_pre, axis=0).reshape(ff_rows, width),
        ],
        axis=0,
    )
    def pair_square(left, right):
        return jnp.sum(exact("ia,ja->ij", left, left) * exact("ib,jb->ij", right, right))

    query_scaled = query_rep * 0.125
    gmix_heads = all_gmix.reshape(n_dev, HEADS, HEAD_DIM)
    square_total = (
        pair_square(all_hid, all_pred)
        + pair_square(all_act, all_branch)
        + pair_square(all_two, all_pre)
        + pair_square(all_mix, all_attn)
        + jnp.sum(input_rep * input_rep) * jnp.sum(all_query * all_query)
        + jnp.sum(
            jnp.sum(all_key * all_key, axis=1) * jnp.sum(query_scaled * query_scaled, axis=1)
        )
        + jnp.sum(
            exact("iha,jha->hij", all_value, all_value)
            * exact("ihe,jhe->hij", gmix_heads, gmix_heads)
        )
        + jnp.sum(vector_total * vector_total)
    )
    grad_norm = jnp.sqrt(square_total)
    shrink = jnp.minimum(1.0, 1.0 / (grad_norm + 1e-06))

    qkv_left = jnp.concatenate(
        [
            jnp.concatenate([all_query, jnp.zeros((2 * width,), jnp.float32)])[None],
            jnp.pad(
                (jnp.eye(HEADS)[:, :, None] * query_scaled[None]).reshape(HEADS, width),
                ((0, 0), (width, width)),
            ),
            jnp.pad(
                (jnp.eye(HEADS)[None, :, :, None] * gmix_heads[:, None]).reshape(
                    n_dev * HEADS, width
                ),
                ((0, 0), (2 * width, 0)),
            ),
        ],
        axis=0,
    )
    qkv_right = jnp.concatenate(
        [input_rep[None], all_key, all_value.reshape(n_dev * HEADS, width)], axis=0
    )

    def shard(array, size):
        return lax.dynamic_slice_in_dim(array, me * size, size, axis=1)

    qkv_grad = exact("ra,rd->da", shard(qkv_left, qkv_weight.shape[1]), qkv_right)
    out_grad = exact("ra,rd->ad", shard(all_mix, out_weight.shape[0]), all_attn)
    fc1_grad = exact("ra,rd->da", shard(all_pre, fc1_weight.shape[1]), all_two)
    fc2_grad = exact("ra,rd->ad", shard(all_act, fc2_weight.shape[0]), all_branch)
    head_grad = exact("ra,rd->ad", shard(all_hid, head_weight.shape[0]), all_pred)
    vector_grad = shard(vector_total, vectors.shape[1])
    old_moments = (qkv_moment, out_moment, fc1_moment, fc2_moment)
    muon_grads = (qkv_grad, out_grad, fc1_grad, fc2_grad)
    new_moments = tuple(
        (
            momentum_keep * old_mom + shrink * grad_piece
            for old_mom, grad_piece in zip(old_moments, muon_grads)
        )
    )

    def tall_slots(left, right):
        tall = exact("ra,rd->ad", left, right)
        tall = tall.reshape(n_dev, -1, width)
        return jnp.pad(tall, ((0, 0), (0, slot_rows - tall.shape[1]), (0, 0)))

    grad_tall = lax.switch(
        me_ns,
        [
            lambda: tall_slots(qkv_left, qkv_right),
            lambda: tall_slots(all_mix, all_attn),
            lambda: tall_slots(all_pre, all_two),
            lambda: tall_slots(all_act, all_branch),
        ],
    )
    tall = momentum_keep * old_tall.astype(jnp.float32) + shrink * grad_tall
    flat_tall = tall.reshape(n_dev * slot_rows, width)
    gram = exact("rd,re->de", flat_tall, flat_tall)
    moment_norm = jnp.sqrt(jnp.trace(gram))
    scale = 1.0 / (moment_norm + 1e-07)
    newton_poly = newton(gram * (scale * scale))
    mine = lax.dynamic_slice_in_dim(tall, me_dp * n_ns, n_ns, axis=0) * scale
    finished = exact("srd,de->sre", mine, newton_poly)
    finished = swap(n_ns, finished, 6)
    long_sizes = (3 * width, width, hidden_units, hidden_units)
    old_weights = (qkv_weight, out_weight, fc1_weight, fc2_weight)
    updates = (
        finished[0, : qkv_weight.shape[1]].T,
        finished[1, : out_weight.shape[0]],
        finished[2, : fc1_weight.shape[1]].T,
        finished[3, : fc2_weight.shape[0]],
    )
    new_weights = tuple(
        (
            old_weight
            - muon_rate
            * (
                math.sqrt(max(1.0, long_size / width)) * update_piece
                + muon_decay * old_weight
            )
            for old_weight, update_piece, long_size in zip(old_weights, updates, long_sizes)
        )
    )
    head_first_new, head_second_new, head_new = adam_update(
        head_weight, head_first, head_second, shrink * head_grad, head_rate, head_decay
    )
    vector_first_new, vector_second_new, vectors_new = adam_update(
        vectors, vector_first, vector_second, shrink * vector_grad, vector_rate, 0.0
    )
    return (
        hidden,
        patch_grads,
        grad_norm,
        *new_moments,
        *new_weights,
        *(piece.astype(half_type) for piece in new_weights),
        head_first_new,
        head_second_new,
        head_new,
        head_new.astype(half_type),
        vector_first_new,
        vector_second_new,
        vectors_new,
        vectors_new.astype(half_type),
    )


def solution(mesh):
    rows, cols, flat = P(both, None), P(None, both), P(both)
    placed = (
        rows, flat, flat, cols,
        cols, rows, cols, rows, rows, cols,
        cols, rows, cols, rows,
        rows, rows, cols, cols,
    )
    returned = (
        rows, rows, P(),
        cols, rows, cols, rows,
        cols, rows, cols, rows,
        cols, rows, cols, rows,
        rows, rows, rows, rows,
        cols, cols, cols, cols,
    )
    return jax.shard_map(
        functools.partial(local, mesh.shape["dp"], mesh.shape["ns"]),
        mesh=mesh,
        in_specs=placed,
        out_specs=returned,
        check_vma=False,
    )
```
